128 devices in a mesh: lat: 8 (over z, core), lon: 16 (over x, y).
Axes of the slice: x: 4, y: 4, z: 4, core: 2. Of those that a mesh axis runs over, the one named last changes fastest.
Arguments:
- control: float32 [32, 1024, 512], P('lat', 'lon'), may hold values from -1.2 to 1.2
- vert_factor: float32 [4, 128, 128], replicated, may hold values from -0.5 to 0.5
- zonal_factor: float32 [1024, 1024], replicated, may hold values from -0.1875 to 0.1875
- obs_dest: int32 [98304, 1], P(('lat', 'lon')), may hold values from 0 to 127; in each aligned block of 768 rows (0 to 767, 768 to 1535, ...) at most 9 rows name the same one
- obs_cell: int32 [98304], P(('lat', 'lon')), may hold values from 0 to 255
- obs_offset: int32 [98304], P(('lat', 'lon')), may hold values from 0 to 96
- obs_count: int32 [128], P(('lat', 'lon')), may hold values from 384 to 768, as said below
- departure: float32 [98304], P(('lat', 'lon')), may hold values from -6 to 6
- obs_rinv: float32 [98304], P(('lat', 'lon')), may hold values from 0.25 to 4
- obs_weights: float32 [98304, 128], P(('lat', 'lon')), may hold values from 0 to 1
Outputs:
- gradient: float32 [32, 1024, 512], P('lat', 'lon')
The draws below stay inside these ranges and needn't reach their ends.
Inputs may be any that keep to these rules, and one draw needn't show every extreme that they name: Among the 768 observations of one device, at most 9 have the same obs_dest, and some value is taken exactly 9 times on some devices. `obs_count`: some device holds exactly 768 live observations.
All inputs are finite; a program needn't handle non-finite values.
Results may differ from the reference program's by a relative error of at most 0.000068.
Values sent between devices are 32-bit elements; how exact they have to be, the bound alone decides.
A program may use at most 64 MiB of HBM per device.

```python
import math
import jax
import jax.numpy as jnp
import numpy as np
from jax import lax

F = 4
LEV = 128
KW = 32
CLAT = 4
CLON = 64
OBS_DEV = 768
NLAT = 32
NLON = 1024
NOBS = 98304
CAP = 9
N_LON = 16
DEVICES = 128


def draw_obs_count(key, part):
    key_level = jax.random.fold_in(key, 11)
    key_pick = jax.random.fold_in(key, 13)
    counts = jax.random.randint(key_level, (DEVICES,), OBS_DEV // 2, OBS_DEV + 1)
    chosen = jax.random.randint(key_pick, (), 0, DEVICES)
    return counts.at[chosen].set(OBS_DEV).astype(jnp.int32)


def with_ends(entries, own_key, least, top_value):
    shape = entries.shape
    spot = [jax.random.randint(jax.random.fold_in(own_key, axis), (), 0, shape[axis]) for axis in range(len(shape))]
    entries = entries.at[tuple(spot)].set(least)
    longest = shape.index(max(shape))
    spot[longest] = (spot[longest] + 1) % shape[longest]
    return entries.at[tuple(spot)].set(top_value)


def levels(key, extent, shards, smallest, top_value):
    def one(axis_at, parts):
        draws = jax.random.uniform(jax.random.fold_in(jax.random.fold_in(key, 6), axis_at), (parts,), jnp.float32, smallest / len(shards), top_value / len(shards))
        return jnp.repeat(jnp.exp(draws), extent[axis_at] // parts).reshape((-1,) + (1,) * (len(extent) - axis_at - 1))

    loudness = one(*shards[0])
    for cut in shards[1:]:
        loudness = loudness * one(*cut)
    return loudness


def routed_block(rng, own, number, rows, count, top, most, slope):
    sequence = jax.random.permutation(rng, count)
    packed, ordinary = portions_of(count, rows * top, most, slope, True), portions_of(count, rows * top, most, slope, False)
    places = jnp.arange(count)

    def named(sizes, turn):
        used = int((sizes > 0).sum())
        fixed = max(1, used // 4)
        shifted = fixed + (places - fixed + turn * (used - fixed)) % max(1, count - fixed)
        return jnp.zeros((count,), jnp.int32).at[sequence[jnp.where(places < fixed, places, shifted)]].set(jnp.asarray(sizes, jnp.int32))

    sizes = jnp.where(number % 4 == 0, named(packed, number // 4), named(ordinary, number - number // 4 - 1))
    mixed = jax.random.permutation(jax.random.fold_in(own, 3), count)
    donor, sink = mixed[0:count // 2 * 2:2], mixed[1:count // 2 * 2:2]
    slack = jnp.minimum(sizes[donor] - 1, most - sizes[sink]) // 2
    slack = jnp.where((donor == sequence[0]) | (sink == sequence[0]) | (sizes[sink] == 0), 0, jnp.maximum(slack, 0))
    shifted = jax.random.randint(jax.random.fold_in(own, 4), (count // 2,), 0, 1 << 20) % (slack + 1)
    sizes = sizes.at[donor].add(-shifted).at[sink].add(shifted)
    items = jnp.searchsorted(jnp.cumsum(sizes), jnp.arange(rows * top), side="right").astype(jnp.int32)
    listing = items.reshape(top, rows).T
    listing = listing[jax.random.permutation(jax.random.fold_in(own, 1), rows)]
    turn = jax.random.randint(jax.random.fold_in(own, 2), (rows, 1), 0, top)
    return jnp.take_along_axis(listing, (jnp.arange(top)[None, :] + turn) % top, axis=1)


def portions_of(count, total, limit, slope, full):
    portions = [(1 << 20) // math.isqrt(grade ** slope) + 1 for grade in range(1, count + 1)]
    largest = limit if full else min(limit, max(-(-total // count), total * portions[0] // sum(portions)))
    least = 1 if total - largest >= count - 1 else 0
    holding, rest = [largest] + [least] * (count - 1), total - largest - least * (count - 1)
    while rest > 0:
        free = [i for i in range(1, count) if holding[i] < largest] or [i for i in range(1, count) if holding[i] < limit]
        mass, budget = sum([portions[i] for i in free]), rest
        for i in free:
            addition = min(limit - holding[i], max(1, budget * portions[i] // mass), rest)
            holding[i] = holding[i] + addition
            rest = rest - addition
    return np.array(holding)


def noise(rng, shape, scale, most, split=(), held_as=jnp.bfloat16):
    result = scale * jax.random.normal(rng, shape, jnp.float32)
    if split:
        result = result * levels(rng, shape, split, -0.22, 0.18)
    return jnp.clip(result, -most, most).astype(held_as)


def setup_inputs(seed: int = 0) -> dict:
    key_of = jax.random.split(jax.random.key(seed), 11)
    control = noise(key_of[0], (NLAT, NLON, F * LEV), 0.2, 1.2, ((0, 8), (1, 16)), jnp.float32)
    vert_factor = noise(key_of[1], (F, LEV, LEV), LEV ** -0.5, 0.5, (), jnp.float32)
    zonal_factor = noise(key_of[2], (NLON, NLON), NLON ** -0.5, 0.1875, (), jnp.float32)
    obs_dest_keys = jax.random.split(jax.random.fold_in(key_of[3], 1), NOBS // OBS_DEV)
    obs_dest_turns = jax.random.permutation(jax.random.fold_in(key_of[3], 3), NOBS // OBS_DEV)
    obs_dest = jax.vmap(lambda own, number: routed_block(jax.random.fold_in(key_of[3], 2), own, number, OBS_DEV, DEVICES, 1, CAP, 2))(obs_dest_keys, obs_dest_turns).reshape((NOBS, 1))
    obs_cell = with_ends(jax.random.randint(key_of[4], (NOBS,), 0, CLAT * CLON), jax.random.fold_in(key_of[4], 1), 0, (CLAT * CLON) - 1).astype(jnp.int32)
    obs_offset = with_ends(jax.random.randint(key_of[5], (NOBS,), 0, LEV - KW + 1), jax.random.fold_in(key_of[5], 1), 0, LEV - KW).astype(jnp.int32)
    obs_count = draw_obs_count(jax.random.fold_in(key_of[10], 71), 0)
    departure = noise(key_of[7], (NOBS,), 1.0, 6.0, ((0, 128),), jnp.float32)
    obs_rinv = jnp.clip(jnp.exp(math.log(4.0) - 2.7725887 * jax.random.uniform(key_of[8], (NOBS,), jnp.float32) ** levels(key_of[8], (NOBS,), ((0, 128),), -0.2, 0.2)), 0.25, 4.0)
    obs_weights = jnp.clip(1.0 * jax.random.uniform(key_of[9], (NOBS, F * KW), jnp.float32) ** levels(key_of[9], (NOBS, F * KW), ((0, 128),), -0.2, 0.2), 0.0, 1.0)
    return {"control": control, "vert_factor": vert_factor, "zonal_factor": zonal_factor, "obs_dest": obs_dest, "obs_cell": obs_cell, "obs_offset": obs_offset, "obs_count": obs_count, "departure": departure, "obs_rinv": obs_rinv, "obs_weights": obs_weights}


def reference(control, vert_factor, zonal_factor, obs_dest, obs_cell, obs_offset, obs_count, departure, obs_rinv, obs_weights):
    rows = jnp.arange(NOBS, dtype=jnp.int32)
    holder = rows // OBS_DEV
    live = (rows % OBS_DEV) < obs_count[holder]
    scaled = jnp.where(live, obs_rinv * departure, jnp.float32(0.0))
    values = (obs_weights * scaled[:, None]).reshape(NOBS, F, KW)
    dest = obs_dest[:, 0]
    glat = (dest // N_LON) * CLAT + obs_cell // CLON
    glon = (dest % N_LON) * CLON + obs_cell % CLON
    column = (glat * NLON + glon).astype(jnp.int32)
    flat = (column[:, None, None] * (F * LEV)
            + jnp.arange(F, dtype=jnp.int32)[None, :, None] * LEV
            + obs_offset[:, None, None]
            + jnp.arange(KW, dtype=jnp.int32)[None, None, :]).astype(jnp.int32)
    adjoint = jnp.zeros((NLAT * NLON * F * LEV,), jnp.float32).at[flat.reshape(-1)].add(values.reshape(-1))
    adjoint = adjoint.reshape(NLAT, NLON, F, LEV)

    def one_row(pair):
        block, base = pair
        vertical = jnp.einsum("nfk,fkl->nfl", block, vert_factor, precision=lax.Precision.HIGHEST)
        zonal = jnp.einsum("nfl,nm->mfl", vertical, zonal_factor, precision=lax.Precision.HIGHEST)
        return base + zonal.reshape(NLON, F * LEV)

    return lax.map(one_row, (adjoint, control))
```

```python
import functools

import jax
import jax.numpy as jnp
from jax import lax
from jax.experimental import pallas as pl
from jax.experimental.pallas import tpu as pltpu
from jax.sharding import PartitionSpec as P

MESH = pl.DeviceIdType.MESH
F32, BF16, I32 = jnp.float32, jnp.bfloat16, jnp.int32
N_OBS = 768
CHUNKS = N_OBS // 128
SLOTS = 1152
MSG = 12
NT = (((1,), (1,)), ((), ()))


def ring(o):
    return min(o, 4 - o)


def offsets(everywhere):
    found = [
        (z, c, x, y)
        for z in range(4 if everywhere else 1)
        for c in range(2 if everywhere else 1)
        for x in range(4)
        for y in range(4)
        if (z, c, x, y) != (0, 0, 0, 0)
    ]
    return sorted(found, key=lambda o: -(ring(o[0]) + ring(o[2]) + ring(o[3])))


ALL = offsets(True)
BAND = offsets(False)


def peer(la, lo, o):
    z, c, x, y = o
    lat = (la // 2 + z) % 4 * 2 + (la % 2 + c) % 2
    lon = (lo // 4 + x) % 4 * 4 + (lo % 4 + y) % 4
    return lat, lon


def split(x):
    hi = x.astype(BF16)
    return hi, (x - hi.astype(F32)).astype(BF16)


def nt(a, b):
    return lax.dot_general(a, b, NT, preferred_element_type=F32)


def nn(a, b):
    return jnp.dot(a, b, preferred_element_type=F32)


def onehot(rows, index):
    ids = lax.broadcasted_iota(I32, (rows, 128), 0)
    return jnp.where(ids == index, 1.0, 0.0).astype(BF16)


def prepare(count_ref, dest_ref, cell_ref, off_ref, dep_ref, rinv_ref, w_ref, wt, lhs, pt, send):
    lane = lax.broadcasted_iota(I32, (1, 128), 1)
    rows = lax.broadcasted_iota(I32, (128, 128), 0)
    cols = lax.broadcasted_iota(I32, (128, 128), 1)
    before = jnp.concatenate(
        [jnp.where(rows < cols, 1.0, 0.0), jnp.ones((128, 128), F32)], axis=1
    ).astype(BF16)
    earlier = jnp.zeros((128, 128), F32)
    for c in range(CHUNKS):
        at = slice(128 * c, 128 * c + 128)
        dest, cell, off = dest_ref[:, at], cell_ref[:, at], off_ref[:, at]
        scaled = jnp.where(lane + 128 * c < count_ref[0], rinv_ref[:, at] * dep_ref[:, at], 0.0)
        wt[at, :] = w_ref[at, :].T * scaled
        mine = rows == dest
        counts = nn(jnp.where(mine, 1.0, 0.0).astype(BF16), before)
        rank = jnp.sum(jnp.where(mine, counts[:, :128] + earlier, 0.0), axis=0, keepdims=True)
        earlier = earlier + counts[:, 128:]
        rank = rank.astype(I32)
        slot = jnp.where(rank < 8, (dest >> 4) * 128 + rank * 16 + (dest & 15), 1024 + dest)
        pt[:, at] = onehot(SLOTS, slot)
        residue, turn = off & 3, off >> 2
        residue, turn = jnp.broadcast_to(residue, (8, 128)), jnp.broadcast_to(turn, (8, 128))
        shares = []
        for f in range(4):
            part = [wt[pl.ds(128 * c + 32 * f + k, 8, stride=4), :] for k in range(4)]
            for s in range(4):
                x = part[s]
                for e in range(1, 4):
                    x = jnp.where(residue == e, part[(s - e) % 4], x)
                by = turn + jnp.where(residue > s, 1, 0)
                for m in (1, 2, 4):
                    x = jnp.where((by & m) != 0, pltpu.roll(x, m, 0), x)
                shares.append(x)
        hi, lo = split(jnp.concatenate(shares, axis=0))
        lhs[0:128, at] = hi
        lhs[128:256, at] = lo
        ids = lax.broadcasted_iota(I32, (16, 128), 0)
        labels = jnp.where(ids == 0, cell, jnp.where(ids == 1, off, 0)).astype(F32)
        lhs[256:272, at] = labels.astype(BF16)

    for pair in range(4):
        got = nt(lhs[...], pt[256 * pair : 256 * pair + 256, :])
        value = got[0:128] + got[128:256]
        for half in range(2):
            a = 2 * pair + half
            at = slice(128 * half, 128 * half + 128)
            for j in range(16):
                send[pl.ds((a * 16 + j) * 16, 8), :] = value[8 * j : 8 * j + 8, at]
            send[pl.ds(a * 256 + 9, 16, stride=16), :] = jnp.broadcast_to(got[256:257, at], (16, 128))
            send[pl.ds(a * 256 + 10, 16, stride=16), :] = jnp.broadcast_to(got[257:258, at], (16, 128))
    got = nt(lhs[...], pt[1024:1152, :])
    value = got[0:128] + got[128:256]
    sub = lax.broadcasted_iota(I32, (8, 128), 0)
    group = lax.broadcasted_iota(I32, (8, 128), 1) >> 4
    for j in range(16):
        x = value[8 * j : 8 * j + 8]
        for m in (1, 2, 4):
            up = pltpu.roll(pltpu.roll(x, 8 - m, 0), 16 * m, 1)
            down = pltpu.roll(pltpu.roll(x, m, 0), 128 - 16 * m, 1)
            i_bit, a_bit = (sub & m) != 0, (group & m) != 0
            x = jnp.where(i_bit == a_bit, x, jnp.where(a_bit, up, down))
        send[pl.ds(j * 16 + 8, 8, stride=256), :] = x
    cell, off = got[256:257], got[257:258]
    for a in range(8):
        first = pltpu.roll(cell, (128 - 16 * a) % 128, 1) if a else cell
        second = pltpu.roll(off, (144 - 16 * a) % 128, 1) if a != 1 else off
        row = jnp.where(lane < 16, first, second)
        send[pl.ds(a * 256 + 11, 16, stride=16), :] = jnp.broadcast_to(row, (16, 128))


def factors(vert_ref, zf, zhi, zlo, vw):
    @pl.loop(0, 8)
    def _(p):
        rows = pl.ds(pl.multiple_of(p * 128, 128), 128)
        for q in range(8):
            hi, lo = split(zf[128 * q : 128 * q + 128, rows].T)
            zhi[rows, 128 * q : 128 * q + 128] = hi
            zlo[rows, 128 * q : 128 * q + 128] = lo

    for f in range(4):
        v = jnp.concatenate([vert_ref[f, pl.ds(s, 32, stride=4), :] for s in range(4)], axis=0)
        hi, lo = split(v)
        vw[128 * f : 128 * f + 128, 0:128] = hi
        vw[128 * f : 128 * f + 128, 128:256] = lo


def scatter(share, recv, tv, t8, tc, to, t11, am, lm, adj):
    for i in range(8):
        tv[pl.ds(i, 128, stride=8), :] = recv[pl.ds(i, 128, stride=16), :].T
    t8[...] = recv[pl.ds(8, 128, stride=16), :].T
    tc[...] = recv[pl.ds(9, 128, stride=16), :].T
    to[...] = recv[pl.ds(10, 128, stride=16), :].T
    t11[...] = recv[pl.ds(11, 128, stride=16), :].T
    sub = lax.broadcasted_iota(I32, (8, 128), 0)

    def block(b):
        for k in range(9):
            if k < 8:
                v = tv[pl.ds(pl.multiple_of((k * 16 + b) * 8, 8), 8), :]
                cell, off = tc[pl.ds(k * 16 + b, 1), :], to[pl.ds(k * 16 + b, 1), :]
            else:
                v = t8[pl.ds(b, 8, stride=16), :]
                cell, off = t11[pl.ds(b, 1), :], t11[pl.ds(16 + b, 1), :]
            cell, off = cell.astype(I32), off.astype(I32)
            first = (off - share + 3) >> 2
            code = (cell >> 6) * 4 + ((first + 7 - sub) >> 3)
            hi = v.astype(BF16).astype(F32)
            lo = v - hi
            at = slice(128 * k, 128 * k + 128)
            hits = [code == n for n in range(16)]
            am[0:128, at] = jnp.concatenate([jnp.where(h, hi, 0.0) for h in hits], axis=0).astype(BF16)
            am[128:256, at] = jnp.concatenate([jnp.where(h, lo, 0.0) for h in hits], axis=0).astype(BF16)
            lm[:, at] = onehot(64, cell & 63)
        got = nt(am[...], lm[...])
        return got[0:128] + got[128:256]

    @pl.loop(0, 8)
    def _(pair):
        both = jnp.concatenate([block(2 * pair), block(2 * pair + 1)], axis=1)
        hi, lo = split(both)
        at = pl.ds(pl.multiple_of(pair * 128, 128), 128)
        adj[0:128, at] = hi
        adj[128:256, at] = lo


def kernel(
    count_ref, dest_ref, cell_ref, off_ref, dep_ref, rinv_ref, w_ref, vert_ref, z_hbm, control_hbm, out_ref,
    wt, lhs, pt, send, recv, zf, zhi, zlo, vw, tv, t8, tc, to, t11, am, lm, adj, zon, back, control,
    send_sem, recv_sem, send2_sem, recv2_sem, load_sem,
):
    la, lo = lax.axis_index("lat"), lax.axis_index("lon")
    me = la * 16 + lo
    barrier = pltpu.get_barrier_semaphore()
    for o in ALL:
        pl.semaphore_signal(barrier, inc=1, device_id=peer(la, lo, o), device_id_type=MESH)
    load_z = pltpu.make_async_copy(z_hbm, zf, load_sem.at[0])
    load_z.start()
    load_control = pltpu.make_async_copy(control_hbm, control, load_sem.at[1])
    load_control.start()

    prepare(count_ref, dest_ref, cell_ref, off_ref, dep_ref, rinv_ref, w_ref, wt, lhs, pt, send)

    def rows16(p):
        return pl.ds(pl.multiple_of(p * 16, 16), MSG)

    pl.semaphore_wait(barrier, len(ALL))
    copies = []
    for o in ALL:
        to_lat, to_lon = peer(la, lo, o)
        p = to_lat * 16 + to_lon
        copy = pltpu.make_async_remote_copy(
            src_ref=send.at[rows16(p)],
            dst_ref=recv.at[rows16(me)],
            send_sem=send_sem.at[p],
            recv_sem=recv_sem.at[me],
            device_id=(to_lat, to_lon),
            device_id_type=MESH,
        )
        copy.start()
    recv[pl.ds(pl.multiple_of(me * 16, 16), 16), :] = send[pl.ds(pl.multiple_of(me * 16, 16), 16), :]

    load_z.wait()
    factors(vert_ref, zf, zhi, zlo, vw)

    def arrived(step, _):
        p = (me + step) % 128
        pltpu.make_async_remote_copy(
            src_ref=send.at[rows16(p)], dst_ref=recv.at[rows16(p)], send_sem=send_sem.at[p], recv_sem=recv_sem.at[p],
            device_id=(p // 16, p % 16), device_id_type=MESH,
        ).wait_recv()
        return 0

    lax.fori_loop(1, 128, arrived, 0)
    scatter(lo % 4, recv, tv, t8, tc, to, t11, am, lm, adj)

    for n in range(4):
        at = slice(256 * n, 256 * n + 256)
        got = nt(zhi[at, :], adj[...])
        zon[at, :] = got[:, 0:128] + got[:, 128:256] + nt(zlo[at, :], adj[0:128, :])

    def rows64(p):
        return pl.ds(pl.multiple_of(p * 64, 64), 64)

    def returned(p, q):
        return pltpu.make_async_remote_copy(
            src_ref=zon.at[rows64(p)], dst_ref=back.at[rows64(q)], send_sem=send2_sem.at[p], recv_sem=recv2_sem.at[q],
            device_id=(la, p), device_id_type=MESH,
        )

    for o in BAND:
        returned(peer(la, lo, o)[1], lo).start()
    back[rows64(lo), :] = zon[rows64(lo), :]
    load_control.wait()

    def come_back(step, _):
        p = (lo + step) % 16
        returned(p, p).wait_recv()
        return 0

    lax.fori_loop(1, 16, come_back, 0)
    group = lax.broadcasted_iota(I32, (64, 128), 1) >> 5
    for f in range(4):
        parts = [back[64 * (4 * f + s) : 64 * (4 * f + s) + 64, :] for s in range(4)]
        rows = []
        for r in range(4):
            x = parts[0] if r == 0 else pltpu.roll(parts[0], 128 - 32 * r, 1)
            for s in range(1, 4):
                y = parts[s] if s == r else pltpu.roll(parts[s], (32 * (s - r)) % 128, 1)
                x = jnp.where(group == s, y, x)
            rows.append(x)
        hi, low = split(jnp.concatenate(rows, axis=0))
        w = vw[128 * f : 128 * f + 128, :]
        got = nn(hi, w)
        got = got[:, 0:128] + got[:, 128:256] + nn(low, w[:, 0:128])
        out_ref[:, 128 * f : 128 * f + 128] = control[:, 128 * f : 128 * f + 128] + got

    def sent(step, _):
        p = (me + step) % 128
        pltpu.make_async_remote_copy(
            src_ref=send.at[rows16(p)], dst_ref=recv.at[rows16(p)], send_sem=send_sem.at[p], recv_sem=recv_sem.at[p],
            device_id=(p // 16, p % 16), device_id_type=MESH,
        ).wait_send()
        return 0

    lax.fori_loop(1, 128, sent, 0)

    def sent_back(step, _):
        p = (lo + step) % 16
        returned(p, p).wait_send()
        return 0

    lax.fori_loop(1, 16, sent_back, 0)


def per_device(
    control, vert_factor, zonal_factor, obs_dest, obs_cell, obs_offset, obs_count, departure, obs_rinv, obs_weights
):
    vmem = pl.BlockSpec(memory_space=pltpu.VMEM)
    anywhere = pl.BlockSpec(memory_space=pl.ANY)
    out = pl.pallas_call(
        kernel,
        out_shape=jax.ShapeDtypeStruct((256, 512), F32),
        in_specs=[pl.BlockSpec(memory_space=pltpu.SMEM)] + [vmem] * 7 + [anywhere] * 2,
        out_specs=vmem,
        scratch_shapes=[
            pltpu.VMEM((N_OBS, 128), F32),
            pltpu.VMEM((272, N_OBS), BF16),
            pltpu.VMEM((SLOTS, N_OBS), BF16),
            pltpu.VMEM((2048, 128), F32),
            pltpu.VMEM((2048, 128), F32),
            pltpu.VMEM((1024, 1024), F32),
            pltpu.VMEM((1024, 1024), BF16),
            pltpu.VMEM((1024, 1024), BF16),
            pltpu.VMEM((512, 256), BF16),
            pltpu.VMEM((1024, 128), F32),
            pltpu.VMEM((128, 128), F32),
            pltpu.VMEM((128, 128), F32),
            pltpu.VMEM((128, 128), F32),
            pltpu.VMEM((128, 128), F32),
            pltpu.VMEM((256, SLOTS), BF16),
            pltpu.VMEM((64, SLOTS), BF16),
            pltpu.VMEM((256, 1024), BF16),
            pltpu.VMEM((1024, 128), F32),
            pltpu.VMEM((1024, 128), F32),
            pltpu.VMEM((256, 512), F32),
            pltpu.SemaphoreType.DMA((128,)),
            pltpu.SemaphoreType.DMA((128,)),
            pltpu.SemaphoreType.DMA((16,)),
            pltpu.SemaphoreType.DMA((16,)),
            pltpu.SemaphoreType.DMA((2,)),
        ],
        compiler_params=pltpu.CompilerParams(
            collective_id=0, has_side_effects=True, vmem_limit_bytes=48 * 2**20
        ),
        name="gradient",
    )(
        obs_count,
        obs_dest.reshape(1, N_OBS),
        obs_cell.reshape(1, N_OBS),
        obs_offset.reshape(1, N_OBS),
        departure.reshape(1, N_OBS),
        obs_rinv.reshape(1, N_OBS),
        obs_weights,
        vert_factor,
        zonal_factor,
        control.reshape(256, 512),
    )
    return out.reshape(4, 64, 512)


def solution(mesh):
    return jax.shard_map(
        per_device,
        mesh=mesh,
        in_specs=(
            P("lat", "lon", None),
            P(),
            P(),
            P(("lat", "lon"), None),
            P(("lat", "lon")),
            P(("lat", "lon")),
            P(("lat", "lon")),
            P(("lat", "lon")),
            P(("lat", "lon")),
            P(("lat", "lon"), None),
        ),
        out_specs=P("lat", "lon", None),
        check_vma=False,
    )
```

```python
import functools

import jax
import jax.numpy as jnp
from jax import lax
from jax.experimental import pallas as pl
from jax.experimental.pallas import tpu as pltpu
from jax.sharding import PartitionSpec as P

MESH = pl.DeviceIdType.MESH
F32, BF16, I32 = jnp.float32, jnp.bfloat16, jnp.int32
N_OBS = 768
CHUNKS = N_OBS // 128
SLOTS = 1152
MSG = 12
NT = (((1,), (1,)), ((), ()))


def ring(o):
    return min(o, 4 - o)


def offsets():
    found = [(z, c, x, y) for z in range(4) for c in range(2) for x in range(4) for y in range(4)][1:]
    return sorted(found, key=lambda o: ((o[0] + o[2] + o[3]) % 4, -(ring(o[0]) + ring(o[2]) + ring(o[3]))))


ALL = offsets()


def peer(la, lo, o):
    z, c, x, y = o
    lat = (la // 2 + z) % 4 * 2 + (la % 2 + c) % 2
    lon = (lo // 4 + x) % 4 * 4 + (lo % 4 + y) % 4
    return lat, lon


def split(x):
    hi = x.astype(BF16)
    return hi, (x - hi.astype(F32)).astype(BF16)


def nt(a, b):
    return lax.dot_general(a, b, NT, preferred_element_type=F32)


def nn(a, b):
    return jnp.dot(a, b, preferred_element_type=F32)


def onehot(rows, index):
    ids = lax.broadcasted_iota(I32, (rows, 128), 0)
    return jnp.where(ids == index, 1.0, 0.0).astype(BF16)


def swap_groups(x):
    sub = lax.broadcasted_iota(I32, (8, 128), 0)
    group = lax.broadcasted_iota(I32, (8, 128), 1) >> 4
    for m in (1, 2, 4):
        up = pltpu.roll(pltpu.roll(x, 8 - m, 0), 16 * m, 1)
        down = pltpu.roll(pltpu.roll(x, m, 0), 128 - 16 * m, 1)
        i_bit, a_bit = (sub & m) != 0, (group & m) != 0
        x = jnp.where(i_bit == a_bit, x, jnp.where(a_bit, up, down))
    return x


def prepare(count_ref, dest_ref, cell_ref, off_ref, dep_ref, rinv_ref, w_ref, wt, lhs, pt, labels, send):
    lane = lax.broadcasted_iota(I32, (1, 128), 1)
    rows = lax.broadcasted_iota(I32, (128, 128), 0)
    cols = lax.broadcasted_iota(I32, (128, 128), 1)
    before = jnp.concatenate(
        [jnp.where(rows < cols, 1.0, 0.0), jnp.ones((128, 128), F32)], axis=1
    ).astype(BF16)
    earlier = jnp.zeros((128, 128), F32)
    for c in range(CHUNKS):
        at = slice(128 * c, 128 * c + 128)
        dest = dest_ref[:, at]
        cell, off, dep, rinv = (r[at].reshape(1, 128) for r in (cell_ref, off_ref, dep_ref, rinv_ref))
        scaled = jnp.where(lane + 128 * c < count_ref[0], rinv * dep, 0.0)
        wt[at, :] = w_ref[at, :].T * scaled
        mine = rows == dest
        counts = nn(jnp.where(mine, 1.0, 0.0).astype(BF16), before)
        rank = jnp.sum(jnp.where(mine, counts[:, :128] + earlier, 0.0), axis=0, keepdims=True)
        earlier = earlier + counts[:, 128:]
        pt[:, at] = onehot(SLOTS, rank.astype(I32) * 128 + dest)
        residue, turn = off & 3, off >> 2
        residue, turn = jnp.broadcast_to(residue, (8, 128)), jnp.broadcast_to(turn, (8, 128))
        shares = []
        for f in range(4):
            part = [wt[pl.ds(128 * c + 32 * f + k, 8, stride=4), :] for k in range(4)]
            for s in range(4):
                x = part[s]
                for e in range(1, 4):
                    x = jnp.where(residue == e, part[(s - e) % 4], x)
                by = turn + jnp.where(residue > s, 1, 0)
                for m in (1, 2, 4):
                    x = jnp.where((by & m) != 0, pltpu.roll(x, m, 0), x)
                shares.append(x)
        hi, lo = split(jnp.concatenate(shares, axis=0))
        lhs[0:128, at] = hi
        lhs[128:256, at] = lo
        ids = lax.broadcasted_iota(I32, (16, 128), 0)
        lhs[256:272, at] = jnp.where(ids == 0, cell, jnp.where(ids == 1, off, 0)).astype(F32).astype(BF16)

    for k in range(0, 9, 2):
        got = nt(lhs[...], pt[128 * k : min(128 * k + 256, SLOTS), :])
        value = got[0:128] + got[128:256]
        for half in range(2 if k < 8 else 1):
            at = slice(128 * half, 128 * half + 128)
            for j in range(16):
                send[pl.ds(j * 16 + k + half, 8, stride=256), :] = swap_groups(value[8 * j : 8 * j + 8, at])
            labels[pl.ds(k + half, 1), :] = got[256:257, at]
            labels[pl.ds(16 + k + half, 1), :] = got[257:258, at]
    cell, off = swap_groups(labels[0:8, :]), swap_groups(labels[16:24, :])
    cell8, off8 = labels[8:9, :], labels[24:25, :]
    for a in range(8):
        first = pltpu.roll(cell8, (128 - 16 * a) % 128, 1) if a else cell8
        second = pltpu.roll(off8, (144 - 16 * a) % 128, 1) if a != 1 else off8
        last = jnp.where(lane < 16, first, second)
        for at, row in ((9, cell[a : a + 1]), (10, off[a : a + 1]), (11, last)):
            send[pl.ds(a * 256 + at, 16, stride=16), :] = jnp.broadcast_to(row, (16, 128))


def factors(vert_ref, zf, zhi, zlo, vw):
    @pl.loop(0, 8)
    def _(p):
        rows = pl.ds(pl.multiple_of(p * 128, 128), 128)
        for q in range(8):
            hi, lo = split(zf[128 * q : 128 * q + 128, rows].T)
            zhi[rows, 128 * q : 128 * q + 128] = hi
            zlo[rows, 128 * q : 128 * q + 128] = lo

    for f in range(4):
        v = jnp.concatenate([vert_ref[f, pl.ds(s, 32, stride=4), :] for s in range(4)], axis=0)
        hi, lo = split(v)
        vw[128 * f : 128 * f + 128, 0:128] = hi
        vw[128 * f : 128 * f + 128, 128:256] = lo


def scatter(share, base, last, recv, tv, tm, am, lm, acc):
    tiles = 3 if last else 2
    lane = lax.broadcasted_iota(I32, (16, 128), 1)
    for t in range(2):
        value = [recv[pl.ds(base + 4 * t + k, 32, stride=16), :] for k in range(4)]
        tv[128 * t : 128 * t + 128, :] = jnp.concatenate(value, axis=0).T
    for n in range(2):
        by_source = recv[pl.ds(base + 9 + n, 32, stride=16), :]
        labels = jnp.concatenate([by_source, jnp.zeros((96, 128), F32)], axis=0).T
        for t in range(2):
            x = labels[64 * t : 64 * t + 16]
            for k in range(1, 4):
                r = 64 * t + 16 * k
                x = jnp.where(lane < 32 * k, x, pltpu.roll(labels[r : r + 16], 32 * k, 1))
            tm[32 * t + 16 * n : 32 * t + 16 * n + 16, :] = x
    if last:
        tv[256:384, :] = recv[pl.ds(8, 128, stride=16), :].T
        tm[64:192, :] = recv[pl.ds(11, 128, stride=16), :].T
    sub = lax.broadcasted_iota(I32, (8, 128), 0)

    @pl.loop(0, 8)
    def _(pair):
        for half in range(2):
            b = 2 * pair + half
            for t in range(tiles):
                v = tv[pl.ds(128 * t + b, 8, stride=16), :]
                cell, off = tm[pl.ds(32 * t + b, 1), :], tm[pl.ds(32 * t + 16 + b, 1), :]
                cell, off = cell.astype(I32), off.astype(I32)
                first = (off - share + 3) >> 2
                code = (cell >> 6) * 4 + ((first + 7 - sub) >> 3)
                hi = v.astype(BF16).astype(F32)
                lo = v - hi
                k = tiles * half + t
                at = slice(128 * k, 128 * k + 128)
                hits = [code == n for n in range(16)]
                am[0:128, at] = jnp.concatenate([jnp.where(h, hi, 0.0) for h in hits], axis=0).astype(BF16)
                am[128:256, at] = jnp.concatenate([jnp.where(h, lo, 0.0) for h in hits], axis=0).astype(BF16)
                lm[:, at] = onehot(128, (cell & 63) + 64 * half)
        at = slice(0, 256 * tiles)
        acc[pair] += nt(am[:, at], lm[:, at])


def kernel(
    count_ref, dest_hbm, cell_hbm, off_hbm, dep_hbm, rinv_hbm, w_hbm, vert_hbm, z_hbm, control_hbm, out_ref,
    dest_ref, cell_ref, off_ref, dep_ref, rinv_ref, w_ref, vert_ref, zf, control,
    wt, lhs, pt, labels, send, recv, zhi, zlo, vw, tv, tm, am, lm, acc, adj, zon, back,
    send_sem, recv_sem, send2_sem, recv2_sem, load_sem,
):
    la, lo = lax.axis_index("lat"), lax.axis_index("lon")
    z, x, y = la // 2, lo // 4, lo % 4
    barrier = pltpu.get_barrier_semaphore()
    for o in ALL:
        pl.semaphore_signal(barrier, inc=1, device_id=peer(la, lo, o), device_id_type=MESH)
    loads = [
        pltpu.make_async_copy(src, dst, load_sem.at[n])
        for n, (src, dst) in enumerate(
            (
                (w_hbm, w_ref), (dest_hbm, dest_ref), (cell_hbm, cell_ref), (off_hbm, off_ref), (dep_hbm, dep_ref),
                (rinv_hbm, rinv_ref), (vert_hbm, vert_ref), (z_hbm, zf), (control_hbm, control),
            )
        )
    ]
    for load in loads:
        load.start()
    for load in loads[:6]:
        load.wait()

    prepare(count_ref, dest_ref, cell_ref, off_ref, dep_ref, rinv_ref, w_ref, wt, lhs, pt, labels, send)

    def rows16(p):
        return pl.ds(pl.multiple_of(p * 16, 16), MSG)

    def place(x, y, z, c):
        return (x + y + z) % 4 * 32 + (x * 4 + y) * 2 + c

    me = place(x, y, z, la % 2)
    pl.semaphore_wait(barrier, len(ALL))

    def message(p, q, device):
        return pltpu.make_async_remote_copy(
            src_ref=send.at[rows16(p)], dst_ref=recv.at[rows16(q)], send_sem=send_sem.at[p], recv_sem=recv_sem.at[q],
            device_id=device, device_id_type=MESH,
        )

    for o in ALL:
        to_lat, to_lon = peer(la, lo, o)
        message(to_lat * 16 + to_lon, me, (to_lat, to_lon)).start()
    mine = pl.ds(pl.multiple_of((la * 16 + lo) * 16, 16), 16)
    recv[pl.ds(pl.multiple_of(me * 16, 16), 16), :] = send[mine, :]

    for load in loads[6:8]:
        load.wait()
    factors(vert_ref, zf, zhi, zlo, vw)
    acc[...] = jnp.zeros_like(acc)

    other = ((la + 1) % 8, lo)
    for k in range(4):
        key = (x + y + z + 4 - k) % 4

        def arrived(step, _):
            q = key * 32 + (me + step) % 32
            message(q, q, other).wait_recv()
            return 0

        lax.fori_loop(0 if k else 1, 32, arrived, 0)
        scatter(lo % 4, pl.multiple_of(key * 512, 512), k == 3, recv, tv, tm, am, lm, acc)
    for pair in range(8):
        hi, low = split(acc[pair, 0:128, :] + acc[pair, 128:256, :])
        adj[0:128, 128 * pair : 128 * pair + 128] = hi
        adj[128:256, 128 * pair : 128 * pair + 128] = low

    def rows64(p):
        return pl.ds(pl.multiple_of(p * 64, 64), 64)

    def returned(p, q):
        return pltpu.make_async_remote_copy(
            src_ref=zon.at[rows64(p)], dst_ref=back.at[rows64(q)], send_sem=send2_sem.at[p], recv_sem=recv2_sem.at[q],
            device_id=(la, p), device_id_type=MESH,
        )

    for ox in (2, 1, 3, 0):
        to_x = (x + ox) % 4
        at = pl.ds(pl.multiple_of(to_x * 256, 256), 256)
        got = nt(zhi[at, :], adj[...])
        zon[at, :] = got[:, 0:128] + got[:, 128:256] + nt(zlo[at, :], adj[0:128, :])
        for oy in (2, 1, 3, 0):
            if (ox, oy) != (0, 0):
                returned(to_x * 4 + (y + oy) % 4, lo).start()
    back[rows64(lo), :] = zon[rows64(lo), :]
    loads[8].wait()

    group = lax.broadcasted_iota(I32, (64, 128), 1) >> 5
    for ox in (2, 3, 1, 0):
        f = (x + ox) % 4
        for oy in (2, 3, 1, 0):
            if (ox, oy) != (0, 0):
                p = f * 4 + (y + oy) % 4
                returned(p, p).wait_recv()
        parts = [back[pl.ds(pl.multiple_of(f * 256 + 64 * s, 64), 64), :] for s in range(4)]
        rows = []
        for r in range(4):
            got = parts[0] if r == 0 else pltpu.roll(parts[0], 128 - 32 * r, 1)
            for s in range(1, 4):
                turned = parts[s] if s == r else pltpu.roll(parts[s], (32 * (s - r)) % 128, 1)
                got = jnp.where(group == s, turned, got)
            rows.append(got)
        hi, low = split(jnp.concatenate(rows, axis=0))
        at = pl.ds(pl.multiple_of(f * 128, 128), 128)
        w = vw[at, :]
        got = nn(hi, w)
        got = got[:, 0:128] + got[:, 128:256] + nn(low, w[:, 0:128])
        out_ref[:, at] = control[:, at] + got

    def sent(step, _):
        p = (la * 16 + lo + step) % 128
        message(p, p, other).wait_send()
        return 0

    lax.fori_loop(1, 128, sent, 0)

    def sent_back(step, _):
        p = (lo + step) % 16
        returned(p, p).wait_send()
        return 0

    lax.fori_loop(1, 16, sent_back, 0)


def per_device(
    control, vert_factor, zonal_factor, obs_dest, obs_cell, obs_offset, obs_count, departure, obs_rinv, obs_weights
):
    anywhere = pl.BlockSpec(memory_space=pl.ANY)
    out = pl.pallas_call(
        kernel,
        out_shape=jax.ShapeDtypeStruct((256, 512), F32),
        in_specs=[pl.BlockSpec(memory_space=pltpu.SMEM)] + [anywhere] * 9,
        out_specs=pl.BlockSpec(memory_space=pltpu.VMEM),
        scratch_shapes=[
            pltpu.VMEM((1, N_OBS), I32),
            pltpu.VMEM((N_OBS,), I32),
            pltpu.VMEM((N_OBS,), I32),
            pltpu.VMEM((N_OBS,), F32),
            pltpu.VMEM((N_OBS,), F32),
            pltpu.VMEM((N_OBS, 128), F32),
            pltpu.VMEM((4, 128, 128), F32),
            pltpu.VMEM((1024, 1024), F32),
            pltpu.VMEM((256, 512), F32),
            pltpu.VMEM((N_OBS, 128), F32),
            pltpu.VMEM((272, N_OBS), BF16),
            pltpu.VMEM((SLOTS, N_OBS), BF16),
            pltpu.VMEM((32, 128), F32),
            pltpu.VMEM((2048, 128), F32),
            pltpu.VMEM((2048, 128), F32),
            pltpu.VMEM((1024, 1024), BF16),
            pltpu.VMEM((1024, 1024), BF16),
            pltpu.VMEM((512, 256), BF16),
            pltpu.VMEM((384, 128), F32),
            pltpu.VMEM((192, 128), F32),
            pltpu.VMEM((256, 768), BF16),
            pltpu.VMEM((128, 768), BF16),
            pltpu.VMEM((8, 256, 128), F32),
            pltpu.VMEM((256, 1024), BF16),
            pltpu.VMEM((1024, 128), F32),
            pltpu.VMEM((1024, 128), F32),
            pltpu.SemaphoreType.DMA((128,)),
            pltpu.SemaphoreType.DMA((128,)),
            pltpu.SemaphoreType.DMA((16,)),
            pltpu.SemaphoreType.DMA((16,)),
            pltpu.SemaphoreType.DMA((9,)),
        ],
        compiler_params=pltpu.CompilerParams(
            collective_id=0, has_side_effects=True, vmem_limit_bytes=60 * 2**20
        ),
        name="gradient",
    )(
        obs_count,
        obs_dest.reshape(1, N_OBS),
        obs_cell,
        obs_offset,
        departure,
        obs_rinv,
        obs_weights,
        vert_factor,
        zonal_factor,
        control.reshape(256, 512),
    )
    return out.reshape(4, 64, 512)


def solution(mesh):
    return jax.shard_map(
        per_device,
        mesh=mesh,
        in_specs=(
            P("lat", "lon", None),
            P(),
            P(),
            P(("lat", "lon"), None),
            P(("lat", "lon")),
            P(("lat", "lon")),
            P(("lat", "lon")),
            P(("lat", "lon")),
            P(("lat", "lon")),
            P(("lat", "lon"), None),
        ),
        out_specs=P("lat", "lon", None),
        check_vma=False,
    )
```

```python
import functools

import jax
import jax.numpy as jnp
from jax import lax
from jax.experimental import pallas as pl
from jax.experimental.pallas import tpu as pltpu
from jax.sharding import PartitionSpec as P

MESH = pl.DeviceIdType.MESH
F32, BF16, I32 = jnp.float32, jnp.bfloat16, jnp.int32
N_OBS = 768
CHUNKS = N_OBS // 128
SLOTS = 1152
MSG = 12
UNROLL = 8
NT = (((1,), (1,)), ((), ()))


def ring(o):
    return min(o, 4 - o)


def offsets():
    found = [(z, c, x, y) for z in range(4) for c in range(2) for x in range(4) for y in range(4)][1:]
    return sorted(found, key=lambda o: ((o[0] + o[2] + o[3]) % 4, -(ring(o[0]) + ring(o[2]) + ring(o[3]))))


ALL = offsets()


def peer(la, lo, o):
    z, c, x, y = o
    lat = (la // 2 + z) % 4 * 2 + (la % 2 + c) % 2
    lon = (lo // 4 + x) % 4 * 4 + (lo % 4 + y) % 4
    return lat, lon


def split(x):
    hi = x.astype(BF16)
    return hi, (x - hi.astype(F32)).astype(BF16)


def nt(a, b):
    return lax.dot_general(a, b, NT, preferred_element_type=F32)


def nn(a, b):
    return jnp.dot(a, b, preferred_element_type=F32)


def onehot(rows, index):
    ids = lax.broadcasted_iota(I32, (rows, 128), 0)
    return jnp.where(ids == index, 1.0, 0.0).astype(BF16)


def swap_groups(x):
    sub = lax.broadcasted_iota(I32, (8, 128), 0)
    group = lax.broadcasted_iota(I32, (8, 128), 1) >> 4
    for m in (1, 2, 4):
        up = pltpu.roll(pltpu.roll(x, 8 - m, 0), 16 * m, 1)
        down = pltpu.roll(pltpu.roll(x, m, 0), 128 - 16 * m, 1)
        i_bit, a_bit = (sub & m) != 0, (group & m) != 0
        x = jnp.where(i_bit == a_bit, x, jnp.where(a_bit, up, down))
    return x


def prepare(count_ref, dest_ref, cell_ref, off_ref, dep_ref, rinv_ref, w_ref, wt, lhs, pt, labels, send):
    lane = lax.broadcasted_iota(I32, (1, 128), 1)
    rows = lax.broadcasted_iota(I32, (128, 128), 0)
    cols = lax.broadcasted_iota(I32, (128, 128), 1)
    before = jnp.concatenate(
        [jnp.where(rows < cols, 1.0, 0.0), jnp.ones((128, 128), F32)], axis=1
    ).astype(BF16)
    earlier = jnp.zeros((128, 128), F32)
    for c in range(CHUNKS):
        at = slice(128 * c, 128 * c + 128)
        dest = dest_ref[:, at]
        cell, off, dep, rinv = (r[at].reshape(1, 128) for r in (cell_ref, off_ref, dep_ref, rinv_ref))
        scaled = jnp.where(lane + 128 * c < count_ref[0], rinv * dep, 0.0)
        wt[at, :] = w_ref[at, :].T * scaled
        mine = rows == dest
        counts = nn(jnp.where(mine, 1.0, 0.0).astype(BF16), before)
        rank = jnp.sum(jnp.where(mine, counts[:, :128] + earlier, 0.0), axis=0, keepdims=True)
        earlier = earlier + counts[:, 128:]
        pt[:, at] = onehot(SLOTS, rank.astype(I32) * 128 + dest)
        residue, turn = off & 3, off >> 2
        residue, turn = jnp.broadcast_to(residue, (8, 128)), jnp.broadcast_to(turn, (8, 128))
        shares = []
        for f in range(4):
            part = [wt[pl.ds(128 * c + 32 * f + k, 8, stride=4), :] for k in range(4)]
            for s in range(4):
                x = part[s]
                for e in range(1, 4):
                    x = jnp.where(residue == e, part[(s - e) % 4], x)
                by = turn + jnp.where(residue > s, 1, 0)
                for m in (1, 2, 4):
                    x = jnp.where((by & m) != 0, pltpu.roll(x, m, 0), x)
                shares.append(x)
        hi, lo = split(jnp.concatenate(shares, axis=0))
        lhs[0:128, at] = hi
        lhs[128:256, at] = lo
        ids = lax.broadcasted_iota(I32, (16, 128), 0)
        lhs[256:272, at] = jnp.where(ids == 0, cell, jnp.where(ids == 1, off, 0)).astype(F32).astype(BF16)

    for k in range(0, 9, 2):
        got = nt(lhs[...], pt[128 * k : min(128 * k + 256, SLOTS), :])
        value = got[0:128] + got[128:256]
        for half in range(2 if k < 8 else 1):
            at = slice(128 * half, 128 * half + 128)
            for j in range(16):
                send[pl.ds(j * 16 + k + half, 8, stride=256), :] = swap_groups(value[8 * j : 8 * j + 8, at])
            labels[pl.ds(k + half, 1), :] = got[256:257, at]
            labels[pl.ds(16 + k + half, 1), :] = got[257:258, at]
    cell, off = swap_groups(labels[0:8, :]), swap_groups(labels[16:24, :])
    cell8, off8 = labels[8:9, :], labels[24:25, :]
    for a in range(8):
        first = pltpu.roll(cell8, (128 - 16 * a) % 128, 1) if a else cell8
        second = pltpu.roll(off8, (144 - 16 * a) % 128, 1) if a != 1 else off8
        last = jnp.where(lane < 16, first, second)
        for at, row in ((9, cell[a : a + 1]), (10, off[a : a + 1]), (11, last)):
            send[pl.ds(a * 256 + at, 16, stride=16), :] = jnp.broadcast_to(row, (16, 128))


def factors(vert_ref, zf, zhi, zlo, vw):
    @pl.loop(0, 8)
    def _(p):
        rows = pl.ds(pl.multiple_of(p * 128, 128), 128)
        for q in range(8):
            hi, lo = split(zf[128 * q : 128 * q + 128, rows].T)
            zhi[rows, 128 * q : 128 * q + 128] = hi
            zlo[rows, 128 * q : 128 * q + 128] = lo

    for f in range(4):
        v = jnp.concatenate([vert_ref[f, pl.ds(s, 32, stride=4), :] for s in range(4)], axis=0)
        hi, lo = split(v)
        vw[128 * f : 128 * f + 128, 0:128] = hi
        vw[128 * f : 128 * f + 128, 128:256] = lo


def scatter(share, base, last, recv, tv, tm, acc):
    tiles = 3 if last else 2
    lane = lax.broadcasted_iota(I32, (16, 128), 1)
    for t in range(2):
        value = [recv[pl.ds(base + 4 * t + k, 32, stride=16), :] for k in range(4)]
        tv[128 * t : 128 * t + 128, :] = jnp.concatenate(value, axis=0).T
    for n in range(2):
        by_source = recv[pl.ds(base + 9 + n, 32, stride=16), :]
        labels = jnp.concatenate([by_source, jnp.zeros((96, 128), F32)], axis=0).T
        for t in range(2):
            x = labels[64 * t : 64 * t + 16]
            for k in range(1, 4):
                r = 64 * t + 16 * k
                x = jnp.where(lane < 32 * k, x, pltpu.roll(labels[r : r + 16], 32 * k, 1))
            tm[32 * t + 16 * n : 32 * t + 16 * n + 16, :] = x
    if last:
        tv[256:384, :] = recv[pl.ds(8, 128, stride=16), :].T
        tm[64:192, :] = recv[pl.ds(11, 128, stride=16), :].T
    sub = lax.broadcasted_iota(I32, (8, 128), 0)
    place = lax.broadcasted_iota(I32, (16, 128), 0).astype(F32)
    zero = jnp.zeros((16, 128), BF16)
    one = jnp.ones((16, 128), BF16)

    def twice(x):
        return jnp.concatenate([x, x], axis=0)

    def tile(b, t):
        v = tv[pl.ds(128 * t + b, 8, stride=16), :]
        cell, off = tm[pl.ds(32 * t + b, 1), :], tm[pl.ds(32 * t + 16 + b, 1), :]
        cell, off = cell.astype(I32), off.astype(I32)
        first = (off - share + 3) >> 2
        code = ((cell >> 6) * 4 + ((first + 7 - sub) >> 3)).astype(F32)
        code = jnp.concatenate([code, code - 1.0], axis=0).astype(BF16)
        hi, lo = split(twice(v))
        hits = [code == jnp.asarray(2 * n, BF16) for n in range(8)]
        levels = jnp.concatenate([jnp.where(h, x, zero) for x in (hi, lo) for h in hits], axis=0)
        lon = (cell & 63).astype(F32)
        columns = [jnp.where((lon - place - 16.0 * n).astype(BF16) == zero, one, zero) for n in range(4)]
        return levels, jnp.concatenate(columns, axis=0)

    def one_pair(pair, _):
        parts = []
        for half in range(2):
            made = [tile(2 * pair + half, t) for t in range(tiles)]
            levels = jnp.concatenate([m[0] for m in made], axis=1)
            columns = jnp.concatenate([m[1] for m in made], axis=1)
            parts.append(nt(levels, columns))
        acc[pair] += jnp.concatenate(parts, axis=1)
        return 0

    lax.fori_loop(0, 8, one_pair, 0, unroll=UNROLL)


def kernel(
    count_ref, dest_hbm, cell_hbm, off_hbm, dep_hbm, rinv_hbm, w_hbm, vert_hbm, z_hbm, out_ref,
    dest_ref, cell_ref, off_ref, dep_ref, rinv_ref, w_ref, vert_ref, zf,
    wt, lhs, pt, labels, send, recv, zhi, zlo, vw, tv, tm, acc, adj, zon, back,
    send_sem, recv_sem, load_sem,
):
    la, lo = lax.axis_index("lat"), lax.axis_index("lon")
    z, x, y = la // 2, lo // 4, lo % 4
    barrier = pltpu.get_barrier_semaphore()
    for o in ALL:
        pl.semaphore_signal(barrier, inc=1, device_id=peer(la, lo, o), device_id_type=MESH)
    loads = [
        pltpu.make_async_copy(src, dst, load_sem.at[n])
        for n, (src, dst) in enumerate(
            (
                (w_hbm, w_ref), (dest_hbm, dest_ref), (cell_hbm, cell_ref), (off_hbm, off_ref), (dep_hbm, dep_ref),
                (rinv_hbm, rinv_ref), (vert_hbm, vert_ref), (z_hbm, zf),
            )
        )
    ]
    for load in loads:
        load.start()
    for load in loads[:6]:
        load.wait()

    prepare(count_ref, dest_ref, cell_ref, off_ref, dep_ref, rinv_ref, w_ref, wt, lhs, pt, labels, send)

    def rows16(p):
        return pl.ds(pl.multiple_of(p * 16, 16), MSG)

    def place(x, y, z, c):
        return (x + y + z) % 4 * 32 + (x * 4 + y) * 2 + c

    me = place(x, y, z, la % 2)
    pl.semaphore_wait(barrier, len(ALL))

    my_key = (x + y + z) % 4
    other = ((la + 1) % 8, lo)

    def message(src, dst, key, device):
        return pltpu.make_async_remote_copy(
            src_ref=send.at[src], dst_ref=recv.at[dst], send_sem=send_sem.at[0], recv_sem=recv_sem.at[key],
            device_id=device, device_id_type=MESH,
        )

    for o in ALL:
        to_lat, to_lon = peer(la, lo, o)
        message(rows16(to_lat * 16 + to_lon), rows16(me), my_key, (to_lat, to_lon)).start()
    mine = pl.ds(pl.multiple_of((la * 16 + lo) * 16, 16), 16)
    recv[pl.ds(pl.multiple_of(me * 16, 16), 16), :] = send[mine, :]

    for load in loads[6:8]:
        load.wait()
    factors(vert_ref, zf, zhi, zlo, vw)
    acc[...] = jnp.zeros_like(acc)

    for k in range(4):
        key = (my_key + 4 - k) % 4
        together = pl.ds(0, MSG * (32 if k else 31))
        message(together, together, key, other).wait_recv()
        scatter(lo % 4, pl.multiple_of(key * 512, 512), k == 3, recv, tv, tm, acc)
    for pair in range(8):
        hi, low = split(acc[pair, 0:128, :] + acc[pair, 128:256, :])
        adj[0:128, 128 * pair : 128 * pair + 128] = hi
        adj[128:256, 128 * pair : 128 * pair + 128] = low

    def rows64(p):
        return pl.ds(pl.multiple_of(p * 64, 64), 64)

    def returned(src, dst, key, device):
        return pltpu.make_async_remote_copy(
            src_ref=zon.at[src], dst_ref=back.at[dst], send_sem=send_sem.at[1], recv_sem=recv_sem.at[4 + key],
            device_id=device, device_id_type=MESH,
        )

    for ox in (2, 1, 3, 0):
        to_x = (x + ox) % 4
        at = pl.ds(pl.multiple_of(to_x * 256, 256), 256)
        got = nt(zhi[at, :], adj[...])
        zon[at, :] = got[:, 0:128] + got[:, 128:256] + nt(zlo[at, :], adj[0:128, :])
        for oy in (2, 1, 3, 0):
            if (ox, oy) != (0, 0):
                p = to_x * 4 + (y + oy) % 4
                returned(rows64(p), rows64(lo), x, (la, p)).start()
    back[rows64(lo), :] = zon[rows64(lo), :]

    group = lax.broadcasted_iota(I32, (64, 128), 1) >> 5
    for ox in (2, 3, 1, 0):
        f = (x + ox) % 4
        together = pl.ds(0, 256 if ox else 192)
        returned(together, together, f, other).wait_recv()
        parts = [back[pl.ds(pl.multiple_of(f * 256 + 64 * s, 64), 64), :] for s in range(4)]
        rows = []
        for r in range(4):
            got = parts[0] if r == 0 else pltpu.roll(parts[0], 128 - 32 * r, 1)
            for s in range(1, 4):
                turned = parts[s] if s == r else pltpu.roll(parts[s], (32 * (s - r)) % 128, 1)
                got = jnp.where(group == s, turned, got)
            rows.append(got)
        hi, low = split(jnp.concatenate(rows, axis=0))
        at = pl.ds(pl.multiple_of(f * 128, 128), 128)
        w = vw[at, :]
        got = nn(hi, w)
        got = got[:, 0:128] + got[:, 128:256] + nn(low, w[:, 0:128])
        out_ref[:, at] = got

    together = pl.ds(0, MSG * 127)
    message(together, together, 0, other).wait_send()
    together = pl.ds(0, 64 * 15)
    returned(together, together, 0, other).wait_send()


def per_device(
    control, vert_factor, zonal_factor, obs_dest, obs_cell, obs_offset, obs_count, departure, obs_rinv, obs_weights
):
    anywhere = pl.BlockSpec(memory_space=pltpu.HBM)
    out = pl.pallas_call(
        kernel,
        out_shape=jax.ShapeDtypeStruct((256, 512), F32),
        in_specs=[pl.BlockSpec(memory_space=pltpu.SMEM)] + [anywhere] * 8,
        out_specs=pl.BlockSpec(memory_space=pltpu.VMEM),
        scratch_shapes=[
            pltpu.VMEM((1, N_OBS), I32),
            pltpu.VMEM((N_OBS,), I32),
            pltpu.VMEM((N_OBS,), I32),
            pltpu.VMEM((N_OBS,), F32),
            pltpu.VMEM((N_OBS,), F32),
            pltpu.VMEM((N_OBS, 128), F32),
            pltpu.VMEM((4, 128, 128), F32),
            pltpu.VMEM((1024, 1024), F32),
            pltpu.VMEM((N_OBS, 128), F32),
            pltpu.VMEM((272, N_OBS), BF16),
            pltpu.VMEM((SLOTS, N_OBS), BF16),
            pltpu.VMEM((32, 128), F32),
            pltpu.VMEM((2048, 128), F32),
            pltpu.VMEM((2048, 128), F32),
            pltpu.VMEM((1024, 1024), BF16),
            pltpu.VMEM((1024, 1024), BF16),
            pltpu.VMEM((512, 256), BF16),
            pltpu.VMEM((384, 128), F32),
            pltpu.VMEM((192, 128), F32),
            pltpu.VMEM((8, 256, 128), F32),
            pltpu.VMEM((256, 1024), BF16),
            pltpu.VMEM((1024, 128), F32),
            pltpu.VMEM((1024, 128), F32),
            pltpu.SemaphoreType.DMA((2,)),
            pltpu.SemaphoreType.DMA((8,)),
            pltpu.SemaphoreType.DMA((8,)),
        ],
        compiler_params=pltpu.CompilerParams(
            collective_id=0, has_side_effects=True, vmem_limit_bytes=60 * 2**20
        ),
        name="gradient",
    )(
        obs_count,
        obs_dest.reshape(1, N_OBS),
        obs_cell,
        obs_offset,
        departure,
        obs_rinv,
        obs_weights,
        vert_factor,
        zonal_factor,
    )
    return control + out.reshape(4, 64, 512)


def solution(mesh):
    return jax.shard_map(
        per_device,
        mesh=mesh,
        in_specs=(
            P("lat", "lon", None),
            P(),
            P(),
            P(("lat", "lon"), None),
            P(("lat", "lon")),
            P(("lat", "lon")),
            P(("lat", "lon")),
            P(("lat", "lon")),
            P(("lat", "lon")),
            P(("lat", "lon"), None),
        ),
        out_specs=P("lat", "lon", None),
        check_vma=False,
    )
```

```python
import functools

import jax
import jax.numpy as jnp
from jax import lax
from jax.experimental import pallas as pl
from jax.experimental.pallas import tpu as pltpu
from jax.sharding import PartitionSpec as P

MESH = pl.DeviceIdType.MESH
F32, BF16, I32 = jnp.float32, jnp.bfloat16, jnp.int32
N_OBS = 768
CHUNKS = N_OBS // 128
SLOTS = 1152
MSG = 12
UNROLL = 8
NT = (((1,), (1,)), ((), ()))


def ring(o):
    return min(o, 4 - o)


def hops(o):
    return ring(o[0]) + ring(o[2]) + ring(o[3])


def offsets():
    found = [(z, c, x, y) for z in range(4) for c in range(2) for x in range(4) for y in range(4)][1:]
    return sorted(found, key=lambda o: ((o[0] + o[2] + o[3]) % 4, -hops(o)))


ALL = offsets()


def peer(la, lo, o):
    z, c, x, y = o
    lat = (la // 2 + z) % 4 * 2 + (la % 2 + c) % 2
    lon = (lo // 4 + x) % 4 * 4 + (lo % 4 + y) % 4
    return lat, lon


def split(x):
    hi = x.astype(BF16)
    return hi, (x - hi.astype(F32)).astype(BF16)


def nt(a, b):
    return lax.dot_general(a, b, NT, preferred_element_type=F32)


def nn(a, b):
    return jnp.dot(a, b, preferred_element_type=F32)


def onehot(rows, index):
    ids = lax.broadcasted_iota(I32, (rows, 128), 0)
    return jnp.where(ids == index, 1.0, 0.0).astype(BF16)


def swap_groups(x):
    sub = lax.broadcasted_iota(I32, (8, 128), 0)
    group = lax.broadcasted_iota(I32, (8, 128), 1) >> 4
    for m in (1, 2, 4):
        up = pltpu.roll(pltpu.roll(x, 8 - m, 0), 16 * m, 1)
        down = pltpu.roll(pltpu.roll(x, m, 0), 128 - 16 * m, 1)
        i_bit, a_bit = (sub & m) != 0, (group & m) != 0
        x = jnp.where(i_bit == a_bit, x, jnp.where(a_bit, up, down))
    return x


def prepare(count_ref, dest_ref, cell_ref, off_ref, dep_ref, rinv_ref, w_ref, wt, lhs, pt, labels, send):
    lane = lax.broadcasted_iota(I32, (1, 128), 1)
    rows = lax.broadcasted_iota(I32, (128, 128), 0)
    cols = lax.broadcasted_iota(I32, (128, 128), 1)
    before = jnp.concatenate(
        [jnp.where(rows < cols, 1.0, 0.0), jnp.ones((128, 128), F32)], axis=1
    ).astype(BF16)
    earlier = jnp.zeros((128, 128), F32)
    for c in range(CHUNKS):
        at = slice(128 * c, 128 * c + 128)
        dest = dest_ref[:, at]
        cell, off, dep, rinv = (r[at].reshape(1, 128) for r in (cell_ref, off_ref, dep_ref, rinv_ref))
        scaled = jnp.where(lane + 128 * c < count_ref[0], rinv * dep, 0.0)
        wt[at, :] = w_ref[at, :].T * scaled
        mine = rows == dest
        counts = nn(jnp.where(mine, 1.0, 0.0).astype(BF16), before)
        rank = jnp.sum(jnp.where(mine, counts[:, :128] + earlier, 0.0), axis=0, keepdims=True)
        earlier = earlier + counts[:, 128:]
        pt[:, at] = onehot(SLOTS, rank.astype(I32) * 128 + dest)
        residue, turn = off & 3, off >> 2
        residue, turn = jnp.broadcast_to(residue, (8, 128)), jnp.broadcast_to(turn, (8, 128))
        shares = []
        for f in range(4):
            part = [wt[pl.ds(128 * c + 32 * f + k, 8, stride=4), :] for k in range(4)]
            for s in range(4):
                x = part[s]
                for e in range(1, 4):
                    x = jnp.where(residue == e, part[(s - e) % 4], x)
                by = turn + jnp.where(residue > s, 1, 0)
                for m in (1, 2, 4):
                    x = jnp.where((by & m) != 0, pltpu.roll(x, m, 0), x)
                shares.append(x)
        hi, lo = split(jnp.concatenate(shares, axis=0))
        lhs[0:128, at] = hi
        lhs[128:256, at] = lo
        ids = lax.broadcasted_iota(I32, (16, 128), 0)
        lhs[256:272, at] = jnp.where(ids == 0, cell, jnp.where(ids == 1, off, 0)).astype(F32).astype(BF16)

    for k in range(0, 9, 2):
        got = nt(lhs[...], pt[128 * k : min(128 * k + 256, SLOTS), :])
        value = got[0:128] + got[128:256]
        for half in range(2 if k < 8 else 1):
            at = slice(128 * half, 128 * half + 128)
            for j in range(16):
                send[pl.ds(j * 16 + k + half, 8, stride=256), :] = swap_groups(value[8 * j : 8 * j + 8, at])
            labels[pl.ds(k + half, 1), :] = got[256:257, at]
            labels[pl.ds(16 + k + half, 1), :] = got[257:258, at]
    cell, off = swap_groups(labels[0:8, :]), swap_groups(labels[16:24, :])
    cell8, off8 = labels[8:9, :], labels[24:25, :]
    for a in range(8):
        first = pltpu.roll(cell8, (128 - 16 * a) % 128, 1) if a else cell8
        second = pltpu.roll(off8, (144 - 16 * a) % 128, 1) if a != 1 else off8
        last = jnp.where(lane < 16, first, second)
        for at, row in ((9, cell[a : a + 1]), (10, off[a : a + 1]), (11, last)):
            send[pl.ds(a * 256 + at, 16, stride=16), :] = jnp.broadcast_to(row, (16, 128))


def factors(vert_ref, zf, zhi, zlo, vw):
    @pl.loop(0, 8)
    def _(p):
        rows = pl.ds(pl.multiple_of(p * 128, 128), 128)
        for q in range(8):
            hi, lo = split(zf[128 * q : 128 * q + 128, rows].T)
            zhi[rows, 128 * q : 128 * q + 128] = hi
            zlo[rows, 128 * q : 128 * q + 128] = lo

    for f in range(4):
        v = jnp.concatenate([vert_ref[f, pl.ds(s, 32, stride=4), :] for s in range(4)], axis=0)
        hi, lo = split(v)
        vw[128 * f : 128 * f + 128, 0:128] = hi
        vw[128 * f : 128 * f + 128, 128:256] = lo


def scatter(share, base, last, recv, tv, tm, acc):
    tiles = 3 if last else 2
    lane = lax.broadcasted_iota(I32, (16, 128), 1)
    for t in range(2):
        value = [recv[pl.ds(base + 4 * t + k, 32, stride=16), :] for k in range(4)]
        tv[128 * t : 128 * t + 128, :] = jnp.concatenate(value, axis=0).T
    for n in range(2):
        by_source = recv[pl.ds(base + 9 + n, 32, stride=16), :]
        labels = jnp.concatenate([by_source, jnp.zeros((96, 128), F32)], axis=0).T
        for t in range(2):
            x = labels[64 * t : 64 * t + 16]
            for k in range(1, 4):
                r = 64 * t + 16 * k
                x = jnp.where(lane < 32 * k, x, pltpu.roll(labels[r : r + 16], 32 * k, 1))
            tm[32 * t + 16 * n : 32 * t + 16 * n + 16, :] = x
    if last:
        tv[256:384, :] = recv[pl.ds(8, 128, stride=16), :].T
        tm[64:192, :] = recv[pl.ds(11, 128, stride=16), :].T
    sub = lax.broadcasted_iota(I32, (8, 128), 0)
    place = lax.broadcasted_iota(I32, (16, 128), 0).astype(F32)
    zero = jnp.zeros((16, 128), BF16)
    one = jnp.ones((16, 128), BF16)

    def twice(x):
        return jnp.concatenate([x, x], axis=0)

    def tile(b, t):
        v = tv[pl.ds(128 * t + b, 8, stride=16), :]
        cell, off = tm[pl.ds(32 * t + b, 1), :], tm[pl.ds(32 * t + 16 + b, 1), :]
        cell, off = cell.astype(I32), off.astype(I32)
        first = (off - share + 3) >> 2
        code = ((cell >> 6) * 4 + ((first + 7 - sub) >> 3)).astype(F32)
        code = jnp.concatenate([code, code - 1.0], axis=0).astype(BF16)
        hi, lo = split(twice(v))
        hits = [code == jnp.asarray(2 * n, BF16) for n in range(8)]
        levels = jnp.concatenate([jnp.where(h, x, zero) for x in (hi, lo) for h in hits], axis=0)
        lon = (cell & 63).astype(F32)
        columns = [jnp.where((lon - place - 16.0 * n).astype(BF16) == zero, one, zero) for n in range(4)]
        return levels, jnp.concatenate(columns, axis=0)

    def one_pair(pair, _):
        parts = []
        for half in range(2):
            made = [tile(2 * pair + half, t) for t in range(tiles)]
            levels = jnp.concatenate([m[0] for m in made], axis=1)
            columns = jnp.concatenate([m[1] for m in made], axis=1)
            parts.append(nt(levels, columns))
        acc[pair] += jnp.concatenate(parts, axis=1)
        return 0

    lax.fori_loop(0, 8, one_pair, 0, unroll=UNROLL)


def kernel(
    count_ref, dest_hbm, cell_hbm, off_hbm, dep_hbm, rinv_hbm, w_hbm, vert_hbm, z_hbm, out_ref,
    dest_ref, cell_ref, off_ref, dep_ref, rinv_ref, w_ref, vert_ref, zf,
    wt, lhs, pt, labels, send, recv, zhi, zlo, vw, tv, tm, acc, adj, zon, back,
    send_sem, recv_sem, load_sem,
):
    la, lo = lax.axis_index("lat"), lax.axis_index("lon")
    z, x, y = la // 2, lo // 4, lo % 4
    barrier = pltpu.get_barrier_semaphore()
    for o in sorted(ALL, key=hops, reverse=True):
        pl.semaphore_signal(barrier, inc=1, device_id=peer(la, lo, o), device_id_type=MESH)
    loads = [
        pltpu.make_async_copy(src, dst, load_sem.at[n])
        for n, (src, dst) in enumerate(
            (
                (w_hbm, w_ref), (dest_hbm, dest_ref), (cell_hbm, cell_ref), (off_hbm, off_ref), (dep_hbm, dep_ref),
                (rinv_hbm, rinv_ref), (vert_hbm, vert_ref), (z_hbm, zf),
            )
        )
    ]
    for load in loads:
        load.start()
    for load in loads[:6]:
        load.wait()

    prepare(count_ref, dest_ref, cell_ref, off_ref, dep_ref, rinv_ref, w_ref, wt, lhs, pt, labels, send)

    def rows16(p):
        return pl.ds(pl.multiple_of(p * 16, 16), MSG)

    def place(x, y, z, c):
        return (x + y + z) % 4 * 32 + (x * 4 + y) * 2 + c

    me = place(x, y, z, la % 2)
    pl.semaphore_wait(barrier, len(ALL))

    my_key = (x + y + z) % 4
    other = ((la + 1) % 8, lo)

    def message(src, dst, key, device):
        return pltpu.make_async_remote_copy(
            src_ref=send.at[src], dst_ref=recv.at[dst], send_sem=send_sem.at[0], recv_sem=recv_sem.at[key],
            device_id=device, device_id_type=MESH,
        )

    for o in ALL:
        to_lat, to_lon = peer(la, lo, o)
        message(rows16(to_lat * 16 + to_lon), rows16(me), my_key, (to_lat, to_lon)).start()
    mine = pl.ds(pl.multiple_of((la * 16 + lo) * 16, 16), 16)
    recv[pl.ds(pl.multiple_of(me * 16, 16), 16), :] = send[mine, :]

    for load in loads[6:8]:
        load.wait()
    factors(vert_ref, zf, zhi, zlo, vw)
    acc[...] = jnp.zeros_like(acc)

    for k in range(4):
        key = (my_key + 4 - k) % 4
        together = pl.ds(0, MSG * (32 if k else 31))
        message(together, together, key, other).wait_recv()
        scatter(lo % 4, pl.multiple_of(key * 512, 512), k == 3, recv, tv, tm, acc)
    for pair in range(8):
        hi, low = split(acc[pair, 0:128, :] + acc[pair, 128:256, :])
        adj[0:128, 128 * pair : 128 * pair + 128] = hi
        adj[128:256, 128 * pair : 128 * pair + 128] = low

    def rows64(p):
        return pl.ds(pl.multiple_of(p * 64, 64), 64)

    def returned(src, dst, key, device):
        return pltpu.make_async_remote_copy(
            src_ref=zon.at[src], dst_ref=back.at[dst], send_sem=send_sem.at[1], recv_sem=recv_sem.at[4 + key],
            device_id=device, device_id_type=MESH,
        )

    for ox in (2, 1, 3, 0):
        to_x = (x + ox) % 4
        at = pl.ds(pl.multiple_of(to_x * 256, 256), 256)
        got = nt(zhi[at, :], adj[...])
        zon[at, :] = got[:, 0:128] + got[:, 128:256] + nt(zlo[at, :], adj[0:128, :])
        for oy in (2, 1, 3, 0):
            if (ox, oy) != (0, 0):
                p = to_x * 4 + (y + oy) % 4
                returned(rows64(p), rows64(lo), x, (la, p)).start()
    back[rows64(lo), :] = zon[rows64(lo), :]

    group = lax.broadcasted_iota(I32, (64, 128), 1) >> 5
    for ox in (2, 3, 1, 0):
        f = (x + ox) % 4
        together = pl.ds(0, 256 if ox else 192)
        returned(together, together, f, other).wait_recv()
        parts = [back[pl.ds(pl.multiple_of(f * 256 + 64 * s, 64), 64), :] for s in range(4)]
        rows = []
        for r in range(4):
            got = parts[0] if r == 0 else pltpu.roll(parts[0], 128 - 32 * r, 1)
            for s in range(1, 4):
                turned = parts[s] if s == r else pltpu.roll(parts[s], (32 * (s - r)) % 128, 1)
                got = jnp.where(group == s, turned, got)
            rows.append(got)
        hi, low = split(jnp.concatenate(rows, axis=0))
        at = pl.ds(pl.multiple_of(f * 128, 128), 128)
        w = vw[at, :]
        got = nn(hi, w)
        got = got[:, 0:128] + got[:, 128:256] + nn(low, w[:, 0:128])
        out_ref[:, at] = got

    together = pl.ds(0, MSG * 127)
    message(together, together, 0, other).wait_send()
    together = pl.ds(0, 64 * 15)
    returned(together, together, 0, other).wait_send()


def per_device(
    control, vert_factor, zonal_factor, obs_dest, obs_cell, obs_offset, obs_count, departure, obs_rinv, obs_weights
):
    anywhere = pl.BlockSpec(memory_space=pltpu.HBM)
    out = pl.pallas_call(
        kernel,
        out_shape=pltpu.VMEM((256, 512), F32),
        in_specs=[pl.BlockSpec(memory_space=pltpu.SMEM)] + [anywhere] * 8,
        out_specs=pl.BlockSpec(memory_space=pltpu.VMEM),
        scratch_shapes=[
            pltpu.VMEM((1, N_OBS), I32),
            pltpu.VMEM((N_OBS,), I32),
            pltpu.VMEM((N_OBS,), I32),
            pltpu.VMEM((N_OBS,), F32),
            pltpu.VMEM((N_OBS,), F32),
            pltpu.VMEM((N_OBS, 128), F32),
            pltpu.VMEM((4, 128, 128), F32),
            pltpu.VMEM((1024, 1024), F32),
            pltpu.VMEM((N_OBS, 128), F32),
            pltpu.VMEM((272, N_OBS), BF16),
            pltpu.VMEM((SLOTS, N_OBS), BF16),
            pltpu.VMEM((32, 128), F32),
            pltpu.VMEM((2048, 128), F32),
            pltpu.VMEM((2048, 128), F32),
            pltpu.VMEM((1024, 1024), BF16),
            pltpu.VMEM((1024, 1024), BF16),
            pltpu.VMEM((512, 256), BF16),
            pltpu.VMEM((384, 128), F32),
            pltpu.VMEM((192, 128), F32),
            pltpu.VMEM((8, 256, 128), F32),
            pltpu.VMEM((256, 1024), BF16),
            pltpu.VMEM((1024, 128), F32),
            pltpu.VMEM((1024, 128), F32),
            pltpu.SemaphoreType.DMA((2,)),
            pltpu.SemaphoreType.DMA((8,)),
            pltpu.SemaphoreType.DMA((8,)),
        ],
        compiler_params=pltpu.CompilerParams(
            collective_id=0, has_side_effects=True, vmem_limit_bytes=40 * 2**20
        ),
        name="gradient",
    )(
        obs_count,
        *(
            pltpu.with_memory_space_constraint(x, pltpu.HBM)
            for x in (
                obs_dest.reshape(1, N_OBS), obs_cell, obs_offset, departure, obs_rinv, obs_weights,
                vert_factor, zonal_factor,
            )
        )
    )
    return control + out.reshape(4, 64, 512)


def solution(mesh):
    return jax.shard_map(
        per_device,
        mesh=mesh,
        in_specs=(
            P("lat", "lon", None),
            P(),
            P(),
            P(("lat", "lon"), None),
            P(("lat", "lon")),
            P(("lat", "lon")),
            P(("lat", "lon")),
            P(("lat", "lon")),
            P(("lat", "lon")),
            P(("lat", "lon"), None),
        ),
        out_specs=P("lat", "lon", None),
        check_vma=False,
    )
```

```python
import functools

import jax
import jax.numpy as jnp
from jax import lax
from jax.experimental import pallas as pl
from jax.experimental.pallas import tpu as pltpu
from jax.sharding import PartitionSpec as P

MESH = pl.DeviceIdType.MESH
F32, BF16, I32 = jnp.float32, jnp.bfloat16, jnp.int32
N_OBS = 768
CHUNKS = N_OBS // 128
SLOTS = 1152
MSG = 12
UNROLL = 8
NT = (((1,), (1,)), ((), ()))


def ring(o):
    return min(o, 4 - o)


def hops(o):
    return ring(o[0]) + ring(o[2]) + ring(o[3])


def offsets():
    found = [(z, c, x, y) for z in range(4) for c in range(2) for x in range(4) for y in range(4)][1:]
    return sorted(found, key=lambda o: ((2, 1, 3, 0).index((o[0] + o[2] + o[3]) % 4), -hops(o)))


ALL = offsets()


def peer(la, lo, o):
    z, c, x, y = o
    lat = (la // 2 + z) % 4 * 2 + (la % 2 + c) % 2
    lon = (lo // 4 + x) % 4 * 4 + (lo % 4 + y) % 4
    return lat, lon


def split(x):
    hi = x.astype(BF16)
    return hi, (x - hi.astype(F32)).astype(BF16)


def nt(a, b):
    return lax.dot_general(a, b, NT, preferred_element_type=F32)


def nn(a, b):
    return jnp.dot(a, b, preferred_element_type=F32)


def onehot(rows, index):
    ids = lax.broadcasted_iota(I32, (rows, 128), 0)
    return jnp.where(ids == index, 1.0, 0.0).astype(BF16)


def swap_groups(x):
    sub = lax.broadcasted_iota(I32, (8, 128), 0)
    group = lax.broadcasted_iota(I32, (8, 128), 1) >> 4
    for m in (1, 2, 4):
        up = pltpu.roll(pltpu.roll(x, 8 - m, 0), 16 * m, 1)
        down = pltpu.roll(pltpu.roll(x, m, 0), 128 - 16 * m, 1)
        i_bit, a_bit = (sub & m) != 0, (group & m) != 0
        x = jnp.where(i_bit == a_bit, x, jnp.where(a_bit, up, down))
    return x


def prepare(count_ref, dest_ref, cell_ref, off_ref, dep_ref, rinv_ref, w_ref, wt, lhs, pt, labels, send):
    lane = lax.broadcasted_iota(I32, (1, 128), 1)
    rows = lax.broadcasted_iota(I32, (128, 128), 0)
    cols = lax.broadcasted_iota(I32, (128, 128), 1)
    before = jnp.concatenate(
        [jnp.where(rows < cols, 1.0, 0.0), jnp.ones((128, 128), F32)], axis=1
    ).astype(BF16)
    earlier = jnp.zeros((128, 128), F32)
    for c in range(CHUNKS):
        at = slice(128 * c, 128 * c + 128)
        dest = dest_ref[:, at]
        cell, off, dep, rinv = (r[at].reshape(1, 128) for r in (cell_ref, off_ref, dep_ref, rinv_ref))
        scaled = jnp.where(lane + 128 * c < count_ref[0], rinv * dep, 0.0)
        wt[at, :] = w_ref[at, :].T * scaled
        mine = rows == dest
        counts = nn(jnp.where(mine, 1.0, 0.0).astype(BF16), before)
        rank = jnp.sum(jnp.where(mine, counts[:, :128] + earlier, 0.0), axis=0, keepdims=True)
        earlier = earlier + counts[:, 128:]
        pt[:, at] = onehot(SLOTS, rank.astype(I32) * 128 + dest)
        residue, turn = off & 3, off >> 2
        residue, turn = jnp.broadcast_to(residue, (8, 128)), jnp.broadcast_to(turn, (8, 128))
        shares = []
        for f in range(4):
            part = [wt[pl.ds(128 * c + 32 * f + k, 8, stride=4), :] for k in range(4)]
            for s in range(4):
                x = part[s]
                for e in range(1, 4):
                    x = jnp.where(residue == e, part[(s - e) % 4], x)
                by = turn + jnp.where(residue > s, 1, 0)
                for m in (1, 2, 4):
                    x = jnp.where((by & m) != 0, pltpu.roll(x, m, 0), x)
                shares.append(x)
        hi, lo = split(jnp.concatenate(shares, axis=0))
        lhs[0:128, at] = hi
        lhs[128:256, at] = lo
        ids = lax.broadcasted_iota(I32, (16, 128), 0)
        lhs[256:272, at] = jnp.where(ids == 0, cell, jnp.where(ids == 1, off, 0)).astype(F32).astype(BF16)

    for k in range(0, 9, 2):
        got = nt(lhs[...], pt[128 * k : min(128 * k + 256, SLOTS), :])
        value = got[0:128] + got[128:256]
        for half in range(2 if k < 8 else 1):
            at = slice(128 * half, 128 * half + 128)
            for j in range(16):
                send[pl.ds(j * 16 + k + half, 8, stride=256), :] = swap_groups(value[8 * j : 8 * j + 8, at])
            labels[pl.ds(k + half, 1), :] = got[256:257, at]
            labels[pl.ds(16 + k + half, 1), :] = got[257:258, at]
    cell, off = swap_groups(labels[0:8, :]), swap_groups(labels[16:24, :])
    cell8, off8 = labels[8:9, :], labels[24:25, :]
    for a in range(8):
        first = pltpu.roll(cell8, (128 - 16 * a) % 128, 1) if a else cell8
        second = pltpu.roll(off8, (144 - 16 * a) % 128, 1) if a != 1 else off8
        last = jnp.where(lane < 16, first, second)
        for at, row in ((9, cell[a : a + 1]), (10, off[a : a + 1]), (11, last)):
            send[pl.ds(a * 256 + at, 16, stride=16), :] = jnp.broadcast_to(row, (16, 128))


def factors(vert_ref, zf, zhi, zlo, vw):
    @pl.loop(0, 8)
    def _(p):
        rows = pl.ds(pl.multiple_of(p * 128, 128), 128)
        for q in range(8):
            hi, lo = split(zf[128 * q : 128 * q + 128, rows].T)
            zhi[rows, 128 * q : 128 * q + 128] = hi
            zlo[rows, 128 * q : 128 * q + 128] = lo

    for f in range(4):
        v = jnp.concatenate([vert_ref[f, pl.ds(s, 32, stride=4), :] for s in range(4)], axis=0)
        hi, lo = split(v)
        vw[128 * f : 128 * f + 128, 0:128] = hi
        vw[128 * f : 128 * f + 128, 128:256] = lo


def scatter(share, base, last, recv, tv, tm, acc):
    tiles = 3 if last else 2
    lane = lax.broadcasted_iota(I32, (16, 128), 1)
    for t in range(2):
        value = [recv[pl.ds(base + 4 * t + k, 32, stride=16), :] for k in range(4)]
        tv[128 * t : 128 * t + 128, :] = jnp.concatenate(value, axis=0).T
    for n in range(2):
        by_source = recv[pl.ds(base + 9 + n, 32, stride=16), :]
        labels = jnp.concatenate([by_source, jnp.zeros((96, 128), F32)], axis=0).T
        for t in range(2):
            x = labels[64 * t : 64 * t + 16]
            for k in range(1, 4):
                r = 64 * t + 16 * k
                x = jnp.where(lane < 32 * k, x, pltpu.roll(labels[r : r + 16], 32 * k, 1))
            tm[32 * t + 16 * n : 32 * t + 16 * n + 16, :] = x
    if last:
        tv[256:384, :] = recv[pl.ds(8, 128, stride=16), :].T
        tm[64:192, :] = recv[pl.ds(11, 128, stride=16), :].T
    sub = lax.broadcasted_iota(I32, (8, 128), 0)
    place = lax.broadcasted_iota(I32, (16, 128), 0).astype(F32)
    zero = jnp.zeros((16, 128), BF16)
    one = jnp.ones((16, 128), BF16)

    def twice(x):
        return jnp.concatenate([x, x], axis=0)

    def tile(b, t):
        v = tv[pl.ds(128 * t + b, 8, stride=16), :]
        cell, off = tm[pl.ds(32 * t + b, 1), :], tm[pl.ds(32 * t + 16 + b, 1), :]
        cell, off = cell.astype(I32), off.astype(I32)
        first = (off - share + 3) >> 2
        code = ((cell >> 6) * 4 + ((first + 7 - sub) >> 3)).astype(F32)
        code = jnp.concatenate([code, code - 1.0], axis=0).astype(BF16)
        hi, lo = split(twice(v))
        hits = [code == jnp.asarray(2 * n, BF16) for n in range(8)]
        levels = jnp.concatenate([jnp.where(h, x, zero) for x in (hi, lo) for h in hits], axis=0)
        lon = (cell & 63).astype(F32)
        columns = [jnp.where((lon - place - 16.0 * n).astype(BF16) == zero, one, zero) for n in range(4)]
        return levels, jnp.concatenate(columns, axis=0)

    def one_pair(pair, _):
        parts = []
        for half in range(2):
            made = [tile(2 * pair + half, t) for t in range(tiles)]
            levels = jnp.concatenate([m[0] for m in made], axis=1)
            columns = jnp.concatenate([m[1] for m in made], axis=1)
            parts.append(nt(levels, columns))
        acc[pair] += jnp.concatenate(parts, axis=1)
        return 0

    lax.fori_loop(0, 8, one_pair, 0, unroll=UNROLL)


def kernel(
    count_ref, dest_hbm, cell_hbm, off_hbm, dep_hbm, rinv_hbm, w_hbm, vert_hbm, z_hbm, out_ref,
    dest_ref, cell_ref, off_ref, dep_ref, rinv_ref, w_ref, vert_ref, zf,
    wt, lhs, pt, labels, send, recv, zhi, zlo, vw, tv, tm, acc, adj, zon, back,
    send_sem, recv_sem, load_sem,
):
    la, lo = lax.axis_index("lat"), lax.axis_index("lon")
    z, x, y = la // 2, lo // 4, lo % 4
    barrier = pltpu.get_barrier_semaphore()
    loads = [
        pltpu.make_async_copy(src, dst, load_sem.at[n])
        for n, (src, dst) in enumerate(
            (
                (w_hbm, w_ref), (dest_hbm, dest_ref), (cell_hbm, cell_ref), (off_hbm, off_ref), (dep_hbm, dep_ref),
                (rinv_hbm, rinv_ref), (vert_hbm, vert_ref), (z_hbm, zf),
            )
        )
    ]
    for load in loads[:6]:
        load.start()
    for o in sorted(ALL, key=hops, reverse=True):
        pl.semaphore_signal(barrier, inc=1, device_id=peer(la, lo, o), device_id_type=MESH)
    for load in loads[6:]:
        load.start()
    for load in loads[:6]:
        load.wait()

    prepare(count_ref, dest_ref, cell_ref, off_ref, dep_ref, rinv_ref, w_ref, wt, lhs, pt, labels, send)

    def rows16(p):
        return pl.ds(pl.multiple_of(p * 16, 16), MSG)

    def place(x, y, z, c):
        return (x + y + z) % 4 * 32 + (x * 4 + y) * 2 + c

    me = place(x, y, z, la % 2)
    pl.semaphore_wait(barrier, len(ALL))

    my_key = (x + y + z) % 4
    other = ((la + 1) % 8, lo)

    def message(src, dst, key, device):
        return pltpu.make_async_remote_copy(
            src_ref=send.at[src], dst_ref=recv.at[dst], send_sem=send_sem.at[0], recv_sem=recv_sem.at[key],
            device_id=device, device_id_type=MESH,
        )

    for o in ALL:
        to_lat, to_lon = peer(la, lo, o)
        message(rows16(to_lat * 16 + to_lon), rows16(me), my_key, (to_lat, to_lon)).start()
    mine = pl.ds(pl.multiple_of((la * 16 + lo) * 16, 16), 16)
    recv[pl.ds(pl.multiple_of(me * 16, 16), 16), :] = send[mine, :]

    for load in loads[6:8]:
        load.wait()
    factors(vert_ref, zf, zhi, zlo, vw)
    acc[...] = jnp.zeros_like(acc)

    for k in (2, 1, 3, 0):
        key = (my_key + 4 - k) % 4
        together = pl.ds(0, MSG * (32 if k else 31))
        message(together, together, key, other).wait_recv()
        scatter(lo % 4, pl.multiple_of(key * 512, 512), k == 0, recv, tv, tm, acc)
    for pair in range(8):
        hi, low = split(acc[pair, 0:128, :] + acc[pair, 128:256, :])
        adj[0:128, 128 * pair : 128 * pair + 128] = hi
        adj[128:256, 128 * pair : 128 * pair + 128] = low

    def rows64(p):
        return pl.ds(pl.multiple_of(p * 64, 64), 64)

    def returned(src, dst, key, device):
        return pltpu.make_async_remote_copy(
            src_ref=zon.at[src], dst_ref=back.at[dst], send_sem=send_sem.at[1], recv_sem=recv_sem.at[4 + key],
            device_id=device, device_id_type=MESH,
        )

    for ox in (2, 1, 3, 0):
        to_x = (x + ox) % 4
        at = pl.ds(pl.multiple_of(to_x * 256, 256), 256)
        got = nt(zhi[at, :], adj[...])
        zon[at, :] = got[:, 0:128] + got[:, 128:256] + nt(zlo[at, :], adj[0:128, :])
        for oy in (2, 1, 3, 0):
            if (ox, oy) != (0, 0):
                p = to_x * 4 + (y + oy) % 4
                returned(rows64(p), rows64(lo), x, (la, p)).start()
    back[rows64(lo), :] = zon[rows64(lo), :]

    group = lax.broadcasted_iota(I32, (64, 128), 1) >> 5
    for ox in (2, 3, 1, 0):
        f = (x + ox) % 4
        together = pl.ds(0, 256 if ox else 192)
        returned(together, together, f, other).wait_recv()
        parts = [back[pl.ds(pl.multiple_of(f * 256 + 64 * s, 64), 64), :] for s in range(4)]
        rows = []
        for r in range(4):
            got = parts[0] if r == 0 else pltpu.roll(parts[0], 128 - 32 * r, 1)
            for s in range(1, 4):
                turned = parts[s] if s == r else pltpu.roll(parts[s], (32 * (s - r)) % 128, 1)
                got = jnp.where(group == s, turned, got)
            rows.append(got)
        hi, low = split(jnp.concatenate(rows, axis=0))
        at = pl.ds(pl.multiple_of(f * 128, 128), 128)
        w = vw[at, :]
        got = nn(hi, w)
        got = got[:, 0:128] + got[:, 128:256] + nn(low, w[:, 0:128])
        out_ref[:, at] = got

    together = pl.ds(0, MSG * 127)
    message(together, together, 0, other).wait_send()
    together = pl.ds(0, 64 * 15)
    returned(together, together, 0, other).wait_send()


def per_device(
    control, vert_factor, zonal_factor, obs_dest, obs_cell, obs_offset, obs_count, departure, obs_rinv, obs_weights
):
    anywhere = pl.BlockSpec(memory_space=pltpu.HBM)
    out = pl.pallas_call(
        kernel,
        out_shape=pltpu.VMEM((256, 512), F32),
        in_specs=[pl.BlockSpec(memory_space=pltpu.SMEM)] + [anywhere] * 8,
        out_specs=pl.BlockSpec(memory_space=pltpu.VMEM),
        scratch_shapes=[
            pltpu.VMEM((1, N_OBS), I32),
            pltpu.VMEM((N_OBS,), I32),
            pltpu.VMEM((N_OBS,), I32),
            pltpu.VMEM((N_OBS,), F32),
            pltpu.VMEM((N_OBS,), F32),
            pltpu.VMEM((N_OBS, 128), F32),
            pltpu.VMEM((4, 128, 128), F32),
            pltpu.VMEM((1024, 1024), F32),
            pltpu.VMEM((N_OBS, 128), F32),
            pltpu.VMEM((272, N_OBS), BF16),
            pltpu.VMEM((SLOTS, N_OBS), BF16),
            pltpu.VMEM((32, 128), F32),
            pltpu.VMEM((2048, 128), F32),
            pltpu.VMEM((2048, 128), F32),
            pltpu.VMEM((1024, 1024), BF16),
            pltpu.VMEM((1024, 1024), BF16),
            pltpu.VMEM((512, 256), BF16),
            pltpu.VMEM((384, 128), F32),
            pltpu.VMEM((192, 128), F32),
            pltpu.VMEM((8, 256, 128), F32),
            pltpu.VMEM((256, 1024), BF16),
            pltpu.VMEM((1024, 128), F32),
            pltpu.VMEM((1024, 128), F32),
            pltpu.SemaphoreType.DMA((2,)),
            pltpu.SemaphoreType.DMA((8,)),
            pltpu.SemaphoreType.DMA((8,)),
        ],
        compiler_params=pltpu.CompilerParams(
            collective_id=0, has_side_effects=True, vmem_limit_bytes=40 * 2**20
        ),
        name="gradient",
    )(
        obs_count,
        *(
            pltpu.with_memory_space_constraint(x, pltpu.HBM)
            for x in (
                obs_dest.reshape(1, N_OBS), obs_cell, obs_offset, departure, obs_rinv, obs_weights,
                vert_factor, zonal_factor,
            )
        )
    )
    return control + out.reshape(4, 64, 512)


def solution(mesh):
    return jax.shard_map(
        per_device,
        mesh=mesh,
        in_specs=(
            P("lat", "lon", None),
            P(),
            P(),
            P(("lat", "lon"), None),
            P(("lat", "lon")),
            P(("lat", "lon")),
            P(("lat", "lon")),
            P(("lat", "lon")),
            P(("lat", "lon")),
            P(("lat", "lon"), None),
        ),
        out_specs=P("lat", "lon", None),
        check_vma=False,
    )
```
